32 devices in a mesh: dp: 8 (over z, y), seq: 4 (over x, core).
Axes of the slice: x: 2, y: 2, z: 4, core: 2. Of those that a mesh axis runs over, the one named last changes fastest.
Arguments:
- tokens: bfloat16 [16, 2048, 768], P('dp', 'seq'), may hold values from -6 to 6
- cotangent: bfloat16 [16, 2048, 768], P('dp', 'seq'), may hold values from -6 to 6
- lengths: int32 [16], replicated, may hold values from 513 to 1984, as said below
- norm_gains: float32 [768, 2], P(('dp', 'seq')), may hold values from 0.1 to 1.9
- shift_taps: float32 [768, 64], P(('dp', 'seq')), may hold values from -0.75 to 0.75
- decay_rate: float32 [768, 32], P(('dp', 'seq')), may hold values from 0.0001 to 0.05
- frequency: float32 [768, 32], P(('dp', 'seq')), may hold values from 0 to 1
- mode_coef: float32 [768, 2, 32], P(('dp', 'seq')), may hold values from -0.036 to 0.036
- skip_gain: float32 [768], P(('dp', 'seq')), may hold values from -6 to 6
- qkv_weight: bfloat16 [768, 2304], P(('dp', 'seq')), may hold values from -0.21875 to 0.21875
- out_weight: bfloat16 [768, 768], P(('dp', 'seq')), may hold values from -0.21875 to 0.21875
- up_weight: bfloat16 [768, 3072], P(('dp', 'seq')), may hold values from -0.21875 to 0.21875
- down_weight: bfloat16 [3072, 768], P(('dp', 'seq')), may hold values from -0.109375 to 0.109375
Outputs:
- layer_out: bfloat16 [16, 2048, 768], P('dp', 'seq')
- input_grad: float32 [16, 2048, 768], P('dp', 'seq')
- norm_gains_grad: float32 [768, 2], P(('dp', 'seq'))
- shift_taps_grad: float32 [768, 64], P(('dp', 'seq'))
- decay_rate_grad: float32 [768, 32], P(('dp', 'seq'))
- frequency_grad: float32 [768, 32], P(('dp', 'seq'))
- mode_coef_grad: float32 [768, 2, 32], P(('dp', 'seq'))
- skip_gain_grad: float32 [768], P(('dp', 'seq'))
- qkv_weight_grad: float32 [768, 2304], P(('dp', 'seq'))
- out_weight_grad: float32 [768, 768], P(('dp', 'seq'))
- up_weight_grad: float32 [768, 3072], P(('dp', 'seq'))
- down_weight_grad: float32 [3072, 768], P(('dp', 'seq'))
The draws below stay inside these ranges and needn't reach their ends.
Inputs may be any that keep to these rules, and one draw needn't show every extreme that they name: `lengths`: slots 2i and 2i + 1 together hold exactly 40 blocks of 64 positions that contain a live position, a partly live block counting as one.
All inputs are finite; a program needn't handle non-finite values.
Results may differ from the reference program's by a relative error of at most 0.011.
Values may be sent and summed in bfloat16 or wider, within the bound.
A program may use at most 192 MiB of HBM per device.

```python
import math
import jax
import jax.numpy as jnp
from jax import lax

D = 768
FF = 3072
STATE = 64
MODES = 32
SLOT = 2048
BLK = 64
NSEQ = 16


def draw_lengths(key, part):
    pair_total = NSEQ // 2
    slot_blocks = SLOT // BLK
    least_blocks = slot_blocks // 4 + 1
    key_blocks, key_trims = jax.random.split(jax.random.fold_in(key, 11))
    leading = jax.random.randint(key_blocks, (pair_total,), least_blocks, slot_blocks, dtype=jnp.int32)
    leading = leading.at[0].set(slot_blocks - 1)
    trailing = 5 * slot_blocks // 4 - leading
    blocks_used = jnp.stack([leading, trailing], axis=1).reshape(NSEQ)
    trims = jax.random.randint(key_trims, (NSEQ,), 0, BLK, dtype=jnp.int32)
    trims = trims.at[0].set(0).at[1].set(BLK - 1)
    return (blocks_used * BLK - trims).astype(jnp.int32)


def shard_levels(rng, dims, cuts, least, top_value):
    level, own = 1.0, jax.random.fold_in(rng, 6)
    for dim, blocks in cuts:
        heights = jnp.exp(jax.random.uniform(jax.random.fold_in(own, dim), (blocks,), jnp.float32, least / len(cuts), top_value / len(cuts)))
        level = level * jnp.repeat(heights, dims[dim] // blocks).reshape([-1 if axis == dim else 1 for axis in range(len(dims))])
    return level


def centred(own_key, extent, deviation, limit, cuts=(), kind=jnp.bfloat16):
    drawn = deviation * jax.random.normal(own_key, extent, jnp.float32)
    if cuts:
        drawn = drawn * shard_levels(own_key, extent, cuts, -0.22, 0.18)
    return jnp.clip(drawn, -limit, limit).astype(kind)


def setup_inputs(seed: int = 0) -> dict:
    key_of = jax.random.split(jax.random.key(seed), 14)
    tokens = centred(key_of[0], (NSEQ, SLOT, D), 1.0, 6.0, ((0, 8), (1, 4)))
    cotangent = centred(key_of[1], (NSEQ, SLOT, D), 1.0, 6.0, ((0, 8), (1, 4)))
    lengths = draw_lengths(jax.random.fold_in(key_of[13], 71), 0)
    norm_gains = jnp.clip(1.0 + 0.18 * jax.random.normal(key_of[3], (D, 2), jnp.float32), 0.1, 1.9)
    shift_taps = centred(key_of[4], (D, STATE), STATE ** -0.5, 0.75, ((0, 32),), jnp.float32)
    decay_rate = jnp.clip(jnp.exp(math.log(0.05) - 6.214608 * jax.random.uniform(key_of[5], (D, MODES), jnp.float32) ** shard_levels(key_of[5], (D, MODES), ((0, 32),), -0.2, 0.2)), 0.0001, 0.05)
    frequency = jnp.clip(1.0 * jax.random.uniform(key_of[6], (D, MODES), jnp.float32) ** shard_levels(key_of[6], (D, MODES), ((0, 32),), -0.2, 0.2), 0.0, 1.0)
    mode_coef = centred(key_of[7], (D, 2, MODES), 0.006, 0.036, ((0, 32),), jnp.float32)
    skip_gain = centred(key_of[8], (D,), 1.0, 6.0, ((0, 32),), jnp.float32)
    qkv_weight = centred(key_of[9], (D, 3 * D), D ** -0.5, 0.21875, ((0, 32),))
    out_weight = centred(key_of[10], (D, D), D ** -0.5, 0.21875, ((0, 32),))
    up_weight = centred(key_of[11], (D, FF), D ** -0.5, 0.21875, ((0, 32),))
    down_weight = centred(key_of[12], (FF, D), FF ** -0.5, 0.109375, ((0, 32),))
    return dict(tokens=tokens, cotangent=cotangent, lengths=lengths, norm_gains=norm_gains, shift_taps=shift_taps, decay_rate=decay_rate, frequency=frequency, mode_coef=mode_coef, skip_gain=skip_gain, qkv_weight=qkv_weight, out_weight=out_weight, up_weight=up_weight, down_weight=down_weight)


@jax.custom_vjp
def low(v):
    return lax.optimization_barrier(v.astype(jnp.bfloat16)).astype(jnp.float32)

@jax.custom_vjp
def low_back(v):
    return v

def low_keep(v):
    return (low(v), None)

def low_pass(kept, grad):
    return (grad,)

def back_keep(v):
    return (v, None)

def back_low(kept, grad):
    return (low(grad),)
low.defvjp(low_keep, low_pass)
low_back.defvjp(back_keep, back_low)
highest = lax.Precision.HIGHEST

def layer_norm(row_block, gain):
    center = row_block - lax.optimization_barrier(jnp.mean(row_block, axis=-1, keepdims=True))
    spread = lax.optimization_barrier(jnp.mean(center * center, axis=-1, keepdims=True))
    return center * lax.rsqrt(spread + 1e-05) * gain

def mode_kernel(decay_part, freq_part, coef_part, length):
    positions = jnp.arange(length).astype(decay_part.dtype)
    fading = jnp.exp(-decay_part[:, :, None] * positions)
    turning = freq_part[:, :, None] * positions
    wave = coef_part[:, 0, :, None] * jnp.cos(turning) - coef_part[:, 1, :, None] * jnp.sin(turning)
    return lax.optimization_barrier(jnp.sum(fading * wave, axis=1))

def causal_conv(signal, kernel):
    length = signal.shape[-1]
    spectrum = jnp.fft.rfft(signal, n=2 * length, axis=-1) * jnp.fft.rfft(kernel, n=2 * length, axis=-1)[:, None, :]
    return jnp.fft.irfft(spectrum, n=2 * length, axis=-1)[..., :length]

def channel_block(pieces):
    grouped, taps_part, decay_part, freq_part, coef_part, skip_part = pieces
    query, keys_part, values_part = (grouped[0], grouped[1], grouped[2])
    shifted = causal_conv(keys_part, taps_part)
    product = shifted * values_part
    kernel = mode_kernel(decay_part, freq_part, coef_part, keys_part.shape[-1])
    state_out = causal_conv(product, kernel) + skip_part[:, None, None] * product
    return query * state_out

def layer_forward(inputs, norm_gains, shift_taps, decay_rate, frequency, mode_coef, skip_gain, qkv_weight, out_weight, up_weight, down_weight, live_mask):

    def first_section(row_block):
        normed = low(layer_norm(row_block, norm_gains[:, 0]))
        return low(low_back(jnp.dot(normed, qkv_weight, precision=highest)))
    projected = lax.map(jax.checkpoint(first_section), inputs)
    seq_count, length, triple = projected.shape
    width = triple // 3
    group_width = 16
    group_count = width // group_width
    grouped = projected.reshape(seq_count, length, 3, group_count, group_width).transpose(3, 2, 4, 0, 1)
    mixed = lax.map(jax.checkpoint(channel_block), (grouped, shift_taps.reshape(group_count, group_width, -1), decay_rate.reshape(group_count, group_width, -1), frequency.reshape(group_count, group_width, -1), mode_coef.reshape(group_count, group_width, 2, -1), skip_gain.reshape(group_count, group_width)))
    mixed = low(low_back(mixed.reshape(width, seq_count, length).transpose(1, 2, 0)))

    def second_section(pieces):
        row_block, mixed_rows, live_rows = pieces
        hidden = row_block + low_back(jnp.dot(mixed_rows, out_weight, precision=highest))
        normed = low(layer_norm(hidden, norm_gains[:, 1]))
        pre_act = low_back(jnp.dot(normed, up_weight, precision=highest))
        activity = low(jax.nn.gelu(pre_act, approximate=False))
        branch = low_back(jnp.dot(activity, down_weight, precision=highest))
        return live_rows[:, None] * (hidden + branch)
    return lax.map(jax.checkpoint(second_section), (inputs, mixed, live_mask))

def reference(tokens, cotangent, lengths, norm_gains, shift_taps, decay_rate, frequency, mode_coef, skip_gain, qkv_weight, out_weight, up_weight, down_weight):
    live_mask = (jnp.arange(SLOT, dtype=jnp.int32)[None, :] < lengths[:, None]).astype(jnp.float32)

    def wrapped(inputs, gains_in, taps_in, rates_in, freqs_in, coefs_in, skips_in, qkv_in, out_in, up_in, down_in):
        return layer_forward(inputs, gains_in, taps_in, rates_in, freqs_in, coefs_in, skips_in, qkv_in, out_in, up_in, down_in, live_mask)
    result, pullback = jax.vjp(wrapped, tokens.astype(jnp.float32), norm_gains, shift_taps, decay_rate, frequency, mode_coef, skip_gain, qkv_weight.astype(jnp.float32), out_weight.astype(jnp.float32), up_weight.astype(jnp.float32), down_weight.astype(jnp.float32))
    grads = pullback(cotangent.astype(jnp.float32))
    return (result.astype(jnp.bfloat16), grads[0], grads[1], grads[2], grads[3], grads[4], grads[5], grads[6], grads[7], grads[8], grads[9], grads[10])
```

```python
import functools

import jax
import jax.numpy as jnp
import numpy as np
from jax import lax
from jax.experimental import pallas as pl
from jax.experimental.pallas import tpu as pltpu
from jax.sharding import PartitionSpec as P

SLOT = 2048
FINE = 64
highest = lax.Precision.HIGHEST
both = ("dp", "seq")


def layer_norm(row_block, gain):
    center = row_block - jnp.mean(row_block, axis=-1, keepdims=True)
    spread = jnp.mean(center * center, axis=-1, keepdims=True)
    return center * lax.rsqrt(spread + 1e-05) * gain


def exact_gelu(values):
    return jax.nn.gelu(values, approximate=False)


def mat_dot(left, right, contract):
    return lax.dot_general(left, right, (contract, ((), ())), preferred_element_type=jnp.float32)


def wave_table(step):
    order = np.concatenate([np.arange(0, step, 2), np.arange(1, step, 2)])
    turns = (2 * order[:, None] + 1) * np.arange(step)[None, :] % (4 * step)
    angles = turns * (np.pi / (2 * step))
    return np.concatenate([np.cos(angles), -np.sin(angles)], axis=0)


def lanes(index, width):
    return slice(index * width, (index + 1) * width)


def transform(table_ref, source_ref, target_ref):
    rows = target_ref.shape[0]
    chunk = min(rows, 256)

    @pl.loop(0, rows // chunk)
    def _(index):
        window = pl.ds(pl.multiple_of(index * chunk, chunk), chunk)
        target_ref[window, :] = jnp.dot(
            table_ref[window, :], source_ref[...], preferred_element_type=jnp.float32
        ).astype(target_ref.dtype)


def over_bins(step, body):
    chunk = 16
    for half, sign in ((0, 1.0), (1, -1.0)):

        @pl.loop(0, step // (2 * chunk))
        def _(index):
            start = pl.multiple_of(half * (step // 2) + index * chunk, chunk)
            body(sign, pl.ds(start, chunk), pl.ds(pl.multiple_of(step + start, chunk), chunk))


def times(left, right):
    return (left[0] * right[0] - left[1] * right[1], left[0] * right[1] + left[1] * right[0])


def times_conj(left, right):
    return (left[0] * right[0] + left[1] * right[1], left[0] * right[1] - left[1] * right[0])


def plus(left, right):
    return right if left is None else (left[0] + right[0], left[1] + right[1])


def load_bins(ref, real, imag, count, width):
    return [
        (
            ref[real, lanes(i, width)].astype(jnp.float32),
            ref[imag, lanes(i, width)].astype(jnp.float32),
        )
        for i in range(count)
    ]


def store_bins(ref, real, imag, index, width, value):
    ref[real, lanes(index, width)] = value[0].astype(ref.dtype)
    ref[imag, lanes(index, width)] = value[1].astype(ref.dtype)


def with_last(bins, sign):
    out = [bins[0]]
    for before, now in zip(bins[:-1], bins[1:]):
        out.append((now[0] - sign * before[1], now[1] + sign * before[0]))
    return out


def with_next(bins, sign):
    out = []
    for now, after in zip(bins[:-1], bins[1:]):
        out.append((now[0] + sign * after[1], now[1] - sign * after[0]))
    return out + [bins[-1]]


def mix_forward(
    count, step, width,
    table_ref, inverse_ref, query_ref, keys_ref, values_ref, kernel_ref, taps_ref, skip_ref,
    mixed_ref, shifted_ref, state_ref, keys_hat_ref, product_hat_ref, kernel_hat_ref, taps_hat_ref,
    source_ref, spectrum_ref, scaled_ref,
):
    state_taps = taps_ref.shape[0]
    chunk = min(step, 128)
    for i in range(count):
        source_ref[:, lanes(i, width)] = keys_ref[pl.ds(i * step, step), :]
    transform(table_ref, source_ref, spectrum_ref)
    taps_hat_ref[...] = jnp.dot(
        table_ref[:, :state_taps], taps_ref[...], preferred_element_type=jnp.float32
    )

    def shift_bins(sign, real, imag):
        keys = load_bins(spectrum_ref, real, imag, count, width)
        taps = (taps_hat_ref[real, :], taps_hat_ref[imag, :])
        for i, value in enumerate(with_last(keys, sign)):
            store_bins(keys_hat_ref, real, imag, i, width, keys[i])
            store_bins(scaled_ref, real, imag, i, width, times(taps, value))

    over_bins(step, shift_bins)

    @pl.loop(0, step // chunk)
    def _(index):
        start = pl.multiple_of(index * chunk, chunk)
        window = pl.ds(start, chunk)
        block = jnp.dot(
            inverse_ref[window, :], scaled_ref[...], preferred_element_type=jnp.float32
        )
        for i in range(count):
            rows = pl.ds(pl.multiple_of(i * step + start, chunk), chunk)
            shifted = block[:, lanes(i, width)]
            shifted_ref[rows, :] = shifted.astype(shifted_ref.dtype)
            product = shifted * values_ref[rows, :].astype(jnp.float32)
            source_ref[window, lanes(i, width)] = product.astype(source_ref.dtype)

    transform(table_ref, source_ref, spectrum_ref)
    for i in range(count):
        scaled_ref[:step, lanes(i, width)] = kernel_ref[pl.ds(i * step, step), :]
    transform(table_ref, scaled_ref.at[pl.ds(0, step), :], kernel_hat_ref)

    def state_bins(sign, real, imag):
        product = load_bins(spectrum_ref, real, imag, count, width)
        kernel = load_bins(kernel_hat_ref, real, imag, count, width)
        joined = with_last(product, sign)
        for m in range(count):
            store_bins(product_hat_ref, real, imag, m, width, product[m])
            total = None
            for d in range(m + 1):
                total = plus(total, times(kernel[d], joined[m - d]))
            store_bins(scaled_ref, real, imag, m, width, total)

    over_bins(step, state_bins)

    @pl.loop(0, step // chunk)
    def _(index):
        start = pl.multiple_of(index * chunk, chunk)
        window = pl.ds(start, chunk)
        block = jnp.dot(
            inverse_ref[window, :], scaled_ref[...], preferred_element_type=jnp.float32
        )
        for i in range(count):
            rows = pl.ds(pl.multiple_of(i * step + start, chunk), chunk)
            product = shifted_ref[rows, :].astype(jnp.float32) * values_ref[rows, :].astype(
                jnp.float32
            )
            state = block[:, lanes(i, width)] + skip_ref[...] * product
            state_ref[rows, :] = state.astype(state_ref.dtype)
            mixed_ref[rows, :] = (query_ref[rows, :].astype(jnp.float32) * state).astype(
                mixed_ref.dtype
            )


def mix_backward(
    count, step, width,
    table_ref, inverse_ref, grad_ref, query_ref, values_ref, shifted_ref, state_ref,
    keys_hat_ref, product_hat_ref, kernel_hat_ref, taps_hat_ref, skip_ref,
    grad_query_ref, grad_keys_ref, grad_values_ref, grad_kernel_ref, grad_taps_ref, grad_skip_ref,
    source_ref, spectrum_ref, scaled_ref, other_ref, taps_acc_ref,
):
    state_taps = grad_taps_ref.shape[0]
    chunk = min(step, 128)
    grad_skip_ref[...] = jnp.zeros_like(grad_skip_ref)

    @pl.loop(0, step // chunk)
    def _(index):
        start = pl.multiple_of(index * chunk, chunk)
        for i in range(count):
            rows = pl.ds(pl.multiple_of(i * step + start, chunk), chunk)
            grad = grad_ref[rows, :].astype(jnp.float32)
            grad_query_ref[rows, :] = (grad * state_ref[rows, :].astype(jnp.float32)).astype(
                grad_query_ref.dtype
            )
            grad_state = grad * query_ref[rows, :].astype(jnp.float32)
            product = shifted_ref[rows, :].astype(jnp.float32) * values_ref[rows, :].astype(
                jnp.float32
            )
            grad_skip_ref[...] += jnp.sum(grad_state * product, axis=0, keepdims=True)
            source_ref[pl.ds(start, chunk), lanes(i, width)] = grad_state.astype(source_ref.dtype)

    transform(table_ref, source_ref, spectrum_ref)

    def state_bins(sign, real, imag):
        joined = with_next(load_bins(spectrum_ref, real, imag, count, width), sign)
        kernel = load_bins(kernel_hat_ref, real, imag, count, width)
        for i in range(count):
            total = None
            for d in range(count - i):
                total = plus(total, times_conj(kernel[d], joined[i + d]))
            store_bins(scaled_ref, real, imag, i, width, total)
        product = load_bins(product_hat_ref, real, imag, count, width)
        for d in range(count):
            total = None
            for i in range(count - d):
                total = plus(total, times_conj(product[i], joined[i + d]))
            store_bins(other_ref, real, imag, d, width, total)

    over_bins(step, state_bins)

    @pl.loop(0, step // chunk)
    def _(index):
        start = pl.multiple_of(index * chunk, chunk)
        window = pl.ds(start, chunk)
        block = jnp.dot(
            inverse_ref[window, :], other_ref[...], preferred_element_type=jnp.float32
        )
        for i in range(count):
            rows = pl.ds(pl.multiple_of(i * step + start, chunk), chunk)
            grad_kernel_ref[rows, :] = block[:, lanes(i, width)]

    @pl.loop(0, step // chunk)
    def _(index):
        start = pl.multiple_of(index * chunk, chunk)
        window = pl.ds(start, chunk)
        block = jnp.dot(
            inverse_ref[window, :], scaled_ref[...], preferred_element_type=jnp.float32
        )
        for i in range(count):
            rows = pl.ds(pl.multiple_of(i * step + start, chunk), chunk)
            grad_state = grad_ref[rows, :].astype(jnp.float32) * query_ref[rows, :].astype(
                jnp.float32
            )
            grad_product = block[:, lanes(i, width)] + skip_ref[...] * grad_state
            grad_values_ref[rows, :] = (
                grad_product * shifted_ref[rows, :].astype(jnp.float32)
            ).astype(grad_values_ref.dtype)
            source_ref[window, lanes(i, width)] = (
                grad_product * values_ref[rows, :].astype(jnp.float32)
            ).astype(source_ref.dtype)

    transform(table_ref, source_ref, spectrum_ref)

    def shift_bins(sign, real, imag):
        joined = with_next(load_bins(spectrum_ref, real, imag, count, width), sign)
        keys = load_bins(keys_hat_ref, real, imag, count, width)
        taps = (taps_hat_ref[real, :], taps_hat_ref[imag, :])
        total = None
        for i in range(count):
            store_bins(scaled_ref, real, imag, i, width, times_conj(taps, joined[i]))
            total = plus(total, times_conj(keys[i], joined[i]))
        store_bins(taps_acc_ref, real, imag, 0, width, total)

    over_bins(step, shift_bins)
    grad_taps_ref[...] = jnp.dot(
        inverse_ref[:state_taps, :], taps_acc_ref[...], preferred_element_type=jnp.float32
    )

    @pl.loop(0, step // chunk)
    def _(index):
        start = pl.multiple_of(index * chunk, chunk)
        window = pl.ds(start, chunk)
        block = jnp.dot(
            inverse_ref[window, :], scaled_ref[...], preferred_element_type=jnp.float32
        )
        for i in range(count):
            rows = pl.ds(pl.multiple_of(i * step + start, chunk), chunk)
            grad_keys_ref[rows, :] = block[:, lanes(i, width)].astype(grad_keys_ref.dtype)


def mixer_sizes(channels):
    step = min(SLOT, 512)
    width = 128 if channels % 128 == 0 else channels
    return SLOT // step, step, width


def run_forward(query, keys, values, kernel, taps, skip):
    channels = keys.shape[1]
    count, step, width = mixer_sizes(channels)
    table = wave_table(step)
    forward_table = jnp.asarray(table, jnp.bfloat16)
    inverse_table = jnp.asarray(table.T / step, jnp.bfloat16)
    fixed = lambda shape: pl.BlockSpec(shape, lambda j: (0, 0), pipeline_mode=pl.Buffered(1))
    column = lambda rows: pl.BlockSpec((rows, width), lambda j: (0, j))
    wide = pl.BlockSpec((2 * step, count * width), lambda j: (0, j))
    shape = jax.ShapeDtypeStruct
    state_taps = taps.shape[0]
    return pl.pallas_call(
        functools.partial(mix_forward, count, step, width),
        grid=(channels // width,),
        in_specs=[fixed((2 * step, step)), fixed((step, 2 * step))]
        + [column(SLOT)] * 4
        + [column(state_taps), column(1)],
        out_specs=[column(SLOT)] * 3 + [wide] * 3 + [column(2 * step)],
        out_shape=[shape((SLOT, channels), jnp.bfloat16)] * 3
        + [shape((2 * step, count * channels), jnp.bfloat16)] * 3
        + [shape((2 * step, channels), jnp.float32)],
        scratch_shapes=[
            pltpu.VMEM((step, count * width), jnp.bfloat16),
            pltpu.VMEM((2 * step, count * width), jnp.float32),
            pltpu.VMEM((2 * step, count * width), jnp.bfloat16),
        ],
        compiler_params=pltpu.CompilerParams(vmem_limit_bytes=48 << 20),
        name="mix_forward",
    )(forward_table, inverse_table, query, keys, values, kernel, taps, skip)


def run_backward(grad, query, values, saved, skip, state_taps):
    channels = query.shape[1]
    count, step, width = mixer_sizes(channels)
    table = wave_table(step)
    forward_table = jnp.asarray(table, jnp.bfloat16)
    inverse_table = jnp.asarray(table.T / step, jnp.bfloat16)
    fixed = lambda shape: pl.BlockSpec(shape, lambda j: (0, 0), pipeline_mode=pl.Buffered(1))
    column = lambda rows: pl.BlockSpec((rows, width), lambda j: (0, j))
    wide = pl.BlockSpec((2 * step, count * width), lambda j: (0, j))
    shape = jax.ShapeDtypeStruct
    shifted, state, keys_hat, product_hat, kernel_hat, taps_hat = saved
    return pl.pallas_call(
        functools.partial(mix_backward, count, step, width),
        grid=(channels // width,),
        in_specs=[fixed((2 * step, step)), fixed((step, 2 * step))]
        + [column(SLOT)] * 5
        + [wide] * 3
        + [column(2 * step), column(1)],
        out_specs=[column(SLOT)] * 4 + [column(state_taps), column(1)],
        out_shape=[shape((SLOT, channels), jnp.bfloat16)] * 3
        + [
            shape((SLOT, channels), jnp.float32),
            shape((state_taps, channels), jnp.float32),
            shape((1, channels), jnp.float32),
        ],
        scratch_shapes=[
            pltpu.VMEM((step, count * width), jnp.bfloat16),
            pltpu.VMEM((2 * step, count * width), jnp.float32),
            pltpu.VMEM((2 * step, count * width), jnp.bfloat16),
            pltpu.VMEM((2 * step, count * width), jnp.bfloat16),
            pltpu.VMEM((2 * step, width), jnp.bfloat16),
        ],
        compiler_params=pltpu.CompilerParams(vmem_limit_bytes=48 << 20),
        name="mix_backward",
    )(
        forward_table, inverse_table, grad, query, values, shifted, state,
        keys_hat, product_hat, kernel_hat, taps_hat, skip,
    )


def powers(rate, turn, count, stride):
    places = (jnp.arange(count) * stride).astype(jnp.float32)
    fade = jnp.exp(-rate[:, :, None] * places)
    angle = turn[:, :, None] * places
    return fade * jnp.cos(angle), fade * jnp.sin(angle)


def mode_kernel(rate, turn, coef):
    coarse_re, coarse_im = powers(rate, turn, SLOT // FINE, FINE)
    fine_re, fine_im = powers(rate, turn, FINE, 1)
    first, second = coef[:, 0, :, None], coef[:, 1, :, None]
    left = jnp.concatenate(
        [first * coarse_re - second * coarse_im, -first * coarse_im - second * coarse_re], axis=1
    )
    right = jnp.concatenate([fine_re, fine_im], axis=1)
    kernel = jnp.einsum("cna,cnb->cab", left, right, precision=highest)
    return kernel.reshape(rate.shape[0], SLOT)


def mode_grads(rate, turn, coef, grad_kernel):
    modes = rate.shape[1]
    coarse_re, coarse_im = powers(rate, turn, SLOT // FINE, FINE)
    fine_re, fine_im = powers(rate, turn, FINE, 1)
    inner = jnp.arange(FINE).astype(jnp.float32)
    right = jnp.concatenate([fine_re, fine_im, inner * fine_re, inner * fine_im], axis=1)
    blocks = grad_kernel.reshape(rate.shape[0], SLOT // FINE, FINE)
    sums = jnp.einsum("cab,cnb->cna", blocks, right, precision=highest)
    low_re, low_im, slope_re, slope_im = (
        sums[:, i * modes : (i + 1) * modes] for i in range(4)
    )
    outer = (jnp.arange(SLOT // FINE) * FINE).astype(jnp.float32)
    slope_re, slope_im = outer * low_re + slope_re, outer * low_im + slope_im
    zero_re = jnp.sum(coarse_re * low_re - coarse_im * low_im, axis=2)
    zero_im = jnp.sum(coarse_re * low_im + coarse_im * low_re, axis=2)
    one_re = jnp.sum(coarse_re * slope_re - coarse_im * slope_im, axis=2)
    one_im = jnp.sum(coarse_re * slope_im + coarse_im * slope_re, axis=2)
    first, second = coef[:, 0], coef[:, 1]
    grad_coef = jnp.stack([zero_re, -zero_im], axis=1)
    grad_rate = -(first * one_re - second * one_im)
    grad_turn = -(first * one_im + second * one_re)
    return grad_rate, grad_turn, grad_coef


def two_parts(values):
    high = values.astype(jnp.bfloat16)
    return high, (values - high.astype(jnp.float32)).astype(jnp.bfloat16)


def local(
    tokens,
    cotangent,
    lengths,
    norm_gains,
    shift_taps,
    decay_rate,
    frequency,
    mode_coef,
    skip_gain,
    qkv_weight,
    out_weight,
    up_weight,
    down_weight,
):
    parts = lax.axis_size("seq")
    slots, length, width = tokens.shape
    half = parts // slots
    place = lax.axis_index("seq")
    slot, rank = place // half, place % half
    channels = width // half
    state_taps = shift_taps.shape[1]
    gather = functools.partial(lax.all_gather, axis_name=both, axis=0, tiled=True)
    scatter = functools.partial(
        lax.psum_scatter, axis_name=both, scatter_dimension=0, tiled=True
    )

    def swap(values):
        return lax.ppermute(values, "seq", [(i, (i + half) % parts) for i in range(parts)])

    def pick(pair, index):
        return lax.dynamic_index_in_dim(pair, index, 0, keepdims=False)

    def rows_of(pair):
        kept, came = pick(pair, slot), swap(pick(pair, 1 - slot))
        low = jnp.where(slot == 0, kept, came)
        high = jnp.where(slot == 0, came, kept)
        return jnp.concatenate([low, high], axis=0)

    def home_of(rows, dtype):
        pair = rows.reshape(2, length, width)
        kept = pick(pair, slot).astype(dtype)
        came = swap(pick(pair, 1 - slot).astype(jnp.bfloat16)).astype(dtype)
        return jnp.stack(
            [jnp.where(slot == 0, kept, came), jnp.where(slot == 0, came, kept)], axis=0
        )

    token_rows = rows_of(tokens)
    cot_rows = rows_of(cotangent)
    qkv_full = gather(qkv_weight)
    gain_high, gain_low = two_parts(norm_gains)
    skip_high, skip_low = two_parts(skip_gain[:, None])
    kernel_own = mode_kernel(decay_rate, frequency, mode_coef)
    small = jnp.concatenate(
        [
            kernel_own.astype(jnp.bfloat16),
            shift_taps.astype(jnp.bfloat16),
            gain_high,
            gain_low,
            skip_high,
            skip_low,
            jnp.zeros((kernel_own.shape[0], 58), jnp.bfloat16),
        ],
        axis=1,
    )
    small_full = gather(small)
    out_full = gather(out_weight)
    up_full = gather(up_weight)
    down_full = gather(down_weight)
    base = SLOT + state_taps
    extra = small_full[:, base : base + 6].astype(jnp.float32)
    gain_one, gain_two = extra[:, 0] + extra[:, 2], extra[:, 1] + extra[:, 3]
    start = rank * channels
    mine = lax.dynamic_slice_in_dim(small_full, start, channels, 0)
    kernel_mine = mine[:, :SLOT].T
    taps_mine = mine[:, SLOT:base].T
    skip_mine = lax.dynamic_slice_in_dim(extra[:, 4] + extra[:, 5], start, channels, 0)[None, :]

    input_rows = token_rows.astype(jnp.float32)
    normed_one, norm_one_back = jax.vjp(layer_norm, input_rows, gain_one)
    normed_low = normed_one.astype(jnp.bfloat16)
    projected = mat_dot(normed_low, qkv_full, ((1,), (0,))).astype(jnp.bfloat16)

    def shift_rank(values, k):
        pairs = [(i, i // half * half + (i % half + k) % half) for i in range(parts)]
        return lax.ppermute(values, "seq", pairs)

    def to_channels(values, fold):
        rows = values.shape[0]
        by_rank = values.reshape(rows, fold, half, channels)
        pieces = []
        for k in range(half):
            piece = lax.dynamic_index_in_dim(by_rank, (rank + k) % half, 2, keepdims=False)
            pieces.append(piece if k == 0 else shift_rank(piece, k))
        ordered = jnp.stack(
            [
                lax.select_n((rank - i) % half, *pieces) if half > 1 else pieces[0]
                for i in range(half)
            ],
            axis=0,
        )
        ordered = ordered.reshape(half, 2, length, fold, channels)
        return ordered.transpose(1, 0, 2, 3, 4).reshape(SLOT, fold, channels)

    def to_rows(values, fold):
        by_rank = values.reshape(2, half, length, fold, channels)
        pieces = []
        for k in range(half):
            piece = lax.dynamic_index_in_dim(by_rank, (rank + k) % half, 1, keepdims=False)
            piece = piece.reshape(2 * length, fold, channels)
            pieces.append(piece if k == 0 else shift_rank(piece, k))
        ordered = [
            lax.select_n((rank - i) % half, *pieces) if half > 1 else pieces[0]
            for i in range(half)
        ]
        return jnp.concatenate(ordered, axis=2).reshape(2 * length, fold * width)

    triple = to_channels(projected, 3)
    query, keys, values = triple[:, 0], triple[:, 1], triple[:, 2]
    mixed, *saved = run_forward(query, keys, values, kernel_mine, taps_mine, skip_mine)
    mixed_rows = to_rows(mixed, 1)
    hidden = input_rows + mat_dot(mixed_rows, out_full, ((1,), (0,)))
    normed_two, norm_two_back = jax.vjp(layer_norm, hidden, gain_two)
    normed_two_low = normed_two.astype(jnp.bfloat16)
    pre_act = mat_dot(normed_two_low, up_full, ((1,), (0,)))
    activity, gelu_back = jax.vjp(exact_gelu, pre_act)
    activity_low = activity.astype(jnp.bfloat16)
    reach = lax.dynamic_index_in_dim(
        lengths, lax.axis_index("dp") * slots + slot, 0, keepdims=False
    )
    ids = rank * length + jnp.arange(length, dtype=jnp.int32)
    ids = jnp.concatenate([ids, ids + SLOT // 2])
    live_mask = (ids < reach).astype(jnp.float32)[:, None]
    result_rows = live_mask * (hidden + mat_dot(activity_low, down_full, ((1,), (0,))))
    layer_out = home_of(result_rows, jnp.bfloat16)

    grad_sum = live_mask * cot_rows.astype(jnp.float32)
    grad_branch = grad_sum.astype(jnp.bfloat16)
    down_grad = mat_dot(activity_low, grad_branch, ((0,), (0,)))
    grad_act = mat_dot(grad_branch, down_full, ((1,), (1,)))
    grad_pre = gelu_back(grad_act)[0].astype(jnp.bfloat16)
    up_grad = mat_dot(normed_two_low, grad_pre, ((0,), (0,)))
    grad_normed = mat_dot(grad_pre, up_full, ((1,), (1,)))
    grad_hidden_norm, grad_gain_two = norm_two_back(grad_normed)
    grad_hidden = grad_sum + grad_hidden_norm
    up_share = scatter(up_grad)
    down_share = scatter(down_grad)
    grad_mix = grad_hidden.astype(jnp.bfloat16)
    out_grad = mat_dot(mixed_rows, grad_mix, ((0,), (0,)))
    grad_mixed = mat_dot(grad_mix, out_full, ((1,), (1,))).astype(jnp.bfloat16)
    channel_grad = to_channels(grad_mixed, 1)[:, 0]
    grad_query, grad_keys, grad_values, grad_kernel, grad_taps, grad_skip = run_backward(
        channel_grad, query, values, saved, skip_mine, state_taps
    )
    grad_projected = to_rows(jnp.stack([grad_query, grad_keys, grad_values], axis=1), 3)
    qkv_grad = mat_dot(normed_low, grad_projected, ((0,), (0,)))
    grad_normed_one = mat_dot(grad_projected, qkv_full, ((1,), (1,)))
    grad_input_norm, grad_gain_one = norm_one_back(grad_normed_one)
    input_grad = home_of(grad_hidden + grad_input_norm, jnp.float32)

    packed = jnp.concatenate([grad_kernel, grad_taps, grad_skip], axis=0).T
    wide = lax.dynamic_update_slice_in_dim(
        jnp.zeros((width, packed.shape[1]), jnp.float32), packed, start, 0
    )
    wide = jnp.concatenate([wide, grad_gain_one[:, None], grad_gain_two[:, None]], axis=1)
    wide = jnp.pad(wide, ((0, 0), (0, -wide.shape[1] % 128)))
    qkv_share, out_share, small_share = scatter(qkv_grad), scatter(out_grad), scatter(wide)
    grad_rate, grad_turn, grad_coef = mode_grads(
        decay_rate, frequency, mode_coef, small_share[:, :SLOT]
    )
    return (
        layer_out,
        input_grad,
        small_share[:, base + 1 : base + 3],
        small_share[:, SLOT:base],
        grad_rate,
        grad_turn,
        grad_coef,
        small_share[:, base],
        qkv_share,
        out_share,
        up_share,
        down_share,
    )


def solution(mesh):
    return jax.shard_map(
        local,
        mesh=mesh,
        in_specs=(
            P("dp", "seq", None),
            P("dp", "seq", None),
            P(),
            P(("dp", "seq"), None),
            P(("dp", "seq"), None),
            P(("dp", "seq"), None),
            P(("dp", "seq"), None),
            P(("dp", "seq"), None, None),
            P(("dp", "seq")),
            P(("dp", "seq"), None),
            P(("dp", "seq"), None),
            P(("dp", "seq"), None),
            P(("dp", "seq"), None),
        ),
        out_specs=(
            P("dp", "seq", None),
            P("dp", "seq", None),
            P(("dp", "seq"), None),
            P(("dp", "seq"), None),
            P(("dp", "seq"), None),
            P(("dp", "seq"), None),
            P(("dp", "seq"), None, None),
            P(("dp", "seq")),
            P(("dp", "seq"), None),
            P(("dp", "seq"), None),
            P(("dp", "seq"), None),
            P(("dp", "seq"), None),
        ),
        check_vma=False,
    )
```

```python
import functools

import jax
import jax.numpy as jnp
import numpy as np
from jax import lax
from jax.experimental import pallas as pl
from jax.experimental.pallas import tpu as pltpu
from jax.sharding import PartitionSpec as P

SLOT = 2048
FINE = 64
highest = lax.Precision.HIGHEST
both = ("dp", "seq")


def layer_norm(row_block, gain):
    center = row_block - jnp.mean(row_block, axis=-1, keepdims=True)
    spread = jnp.mean(center * center, axis=-1, keepdims=True)
    return center * lax.rsqrt(spread + 1e-05) * gain


def exact_gelu(values):
    return jax.nn.gelu(values, approximate=False)


def mat_dot(left, right, contract):
    return lax.dot_general(left, right, (contract, ((), ())), preferred_element_type=jnp.float32)


def wave_table(step):
    order = np.concatenate([np.arange(0, step, 2), np.arange(1, step, 2)])
    turns = (2 * order[:, None] + 1) * np.arange(step)[None, :] % (4 * step)
    angles = turns * (np.pi / (2 * step))
    return np.concatenate([np.cos(angles), -np.sin(angles)], axis=0)


def lanes(index, width):
    return slice(index * width, (index + 1) * width)


def transform(table_ref, source_ref, target_ref):
    rows = target_ref.shape[0]
    chunk = min(rows, 256)

    @pl.loop(0, rows // chunk)
    def _(index):
        window = pl.ds(pl.multiple_of(index * chunk, chunk), chunk)
        target_ref[window, :] = jnp.dot(
            table_ref[window, :], source_ref[...], preferred_element_type=jnp.float32
        ).astype(target_ref.dtype)


def over_bins(step, body):
    chunk = 16
    for half, sign in ((0, 1.0), (1, -1.0)):

        @pl.loop(0, step // (2 * chunk))
        def _(index):
            start = pl.multiple_of(half * (step // 2) + index * chunk, chunk)
            body(sign, pl.ds(start, chunk), pl.ds(pl.multiple_of(step + start, chunk), chunk))


def times(left, right):
    return (left[0] * right[0] - left[1] * right[1], left[0] * right[1] + left[1] * right[0])


def times_conj(left, right):
    return (left[0] * right[0] + left[1] * right[1], left[0] * right[1] - left[1] * right[0])


def plus(left, right):
    return right if left is None else (left[0] + right[0], left[1] + right[1])


def load_bins(ref, real, imag, count, width):
    return [
        (
            ref[real, lanes(i, width)].astype(jnp.float32),
            ref[imag, lanes(i, width)].astype(jnp.float32),
        )
        for i in range(count)
    ]


def store_bins(ref, real, imag, index, width, value):
    ref[real, lanes(index, width)] = value[0].astype(ref.dtype)
    ref[imag, lanes(index, width)] = value[1].astype(ref.dtype)


def with_last(bins, sign):
    out = [bins[0]]
    for before, now in zip(bins[:-1], bins[1:]):
        out.append((now[0] - sign * before[1], now[1] + sign * before[0]))
    return out


def with_next(bins, sign):
    out = []
    for now, after in zip(bins[:-1], bins[1:]):
        out.append((now[0] + sign * after[1], now[1] - sign * after[0]))
    return out + [bins[-1]]


def mix_forward(
    count, step, width,
    table_ref, inverse_ref, table_low_ref, query_ref, keys_ref, values_ref, kernel_ref, taps_ref, skip_ref,
    mixed_ref, shifted_ref, state_ref, keys_hat_ref, product_hat_ref, kernel_hat_ref, taps_hat_ref,
    source_ref, spectrum_ref, scaled_ref, product_ref,
):
    state_taps = taps_ref.shape[0] // 2
    chunk = min(step, 128)
    for i in range(count):
        source_ref[:, lanes(i, width)] = keys_ref[pl.ds(i * step, step), :]
    transform(table_ref, source_ref, spectrum_ref)
    narrow = table_ref[:, :state_taps]
    taps_hat_ref[...] = (
        jnp.dot(narrow, taps_ref[:state_taps, :], preferred_element_type=jnp.float32)
        + jnp.dot(narrow, taps_ref[state_taps:, :], preferred_element_type=jnp.float32)
        + jnp.dot(table_low_ref[...], taps_ref[:state_taps, :], preferred_element_type=jnp.float32)
    )

    def shift_bins(sign, real, imag):
        keys = load_bins(spectrum_ref, real, imag, count, width)
        taps = (taps_hat_ref[real, :], taps_hat_ref[imag, :])
        for i, value in enumerate(with_last(keys, sign)):
            store_bins(keys_hat_ref, real, imag, i, width, keys[i])
            store_bins(scaled_ref, real, imag, i, width, times(taps, value))

    over_bins(step, shift_bins)

    @pl.loop(0, step // chunk)
    def _(index):
        start = pl.multiple_of(index * chunk, chunk)
        window = pl.ds(start, chunk)
        block = jnp.dot(
            inverse_ref[window, :], scaled_ref[...], preferred_element_type=jnp.float32
        )
        for i in range(count):
            rows = pl.ds(pl.multiple_of(i * step + start, chunk), chunk)
            shifted = block[:, lanes(i, width)]
            shifted_ref[rows, :] = shifted.astype(shifted_ref.dtype)
            product = shifted * values_ref[rows, :].astype(jnp.float32)
            product_ref[rows, :] = product
            source_ref[window, lanes(i, width)] = product.astype(source_ref.dtype)

    transform(table_ref, source_ref, spectrum_ref)
    for i in range(count):
        scaled_ref[:step, lanes(i, width)] = kernel_ref[pl.ds(i * step, step), :]
    transform(table_ref, scaled_ref.at[pl.ds(0, step), :], kernel_hat_ref)

    def state_bins(sign, real, imag):
        product = load_bins(spectrum_ref, real, imag, count, width)
        kernel = load_bins(kernel_hat_ref, real, imag, count, width)
        joined = with_last(product, sign)
        for m in range(count):
            store_bins(product_hat_ref, real, imag, m, width, product[m])
            total = None
            for d in range(m + 1):
                total = plus(total, times(kernel[d], joined[m - d]))
            store_bins(scaled_ref, real, imag, m, width, total)

    over_bins(step, state_bins)

    @pl.loop(0, step // chunk)
    def _(index):
        start = pl.multiple_of(index * chunk, chunk)
        window = pl.ds(start, chunk)
        block = jnp.dot(
            inverse_ref[window, :], scaled_ref[...], preferred_element_type=jnp.float32
        )
        for i in range(count):
            rows = pl.ds(pl.multiple_of(i * step + start, chunk), chunk)
            state = block[:, lanes(i, width)] + skip_ref[...] * product_ref[rows, :]
            state_ref[rows, :] = state.astype(state_ref.dtype)
            mixed_ref[rows, :] = (query_ref[rows, :].astype(jnp.float32) * state).astype(
                mixed_ref.dtype
            )


def mix_backward(
    count, step, width,
    table_ref, inverse_ref, grad_ref, query_ref, values_ref, shifted_ref, state_ref,
    keys_hat_ref, product_hat_ref, kernel_hat_ref, taps_hat_ref, skip_ref,
    grad_query_ref, grad_keys_ref, grad_values_ref, grad_kernel_ref, grad_taps_ref, grad_skip_ref,
    source_ref, spectrum_ref, scaled_ref, other_ref, taps_acc_ref,
):
    state_taps = grad_taps_ref.shape[0]
    chunk = min(step, 128)
    grad_skip_ref[...] = jnp.zeros_like(grad_skip_ref)

    @pl.loop(0, step // chunk)
    def _(index):
        start = pl.multiple_of(index * chunk, chunk)
        for i in range(count):
            rows = pl.ds(pl.multiple_of(i * step + start, chunk), chunk)
            grad = grad_ref[rows, :].astype(jnp.float32)
            grad_query_ref[rows, :] = (grad * state_ref[rows, :].astype(jnp.float32)).astype(
                grad_query_ref.dtype
            )
            grad_state = grad * query_ref[rows, :].astype(jnp.float32)
            product = shifted_ref[rows, :].astype(jnp.float32) * values_ref[rows, :].astype(
                jnp.float32
            )
            grad_skip_ref[...] += jnp.sum(grad_state * product, axis=0, keepdims=True)
            source_ref[pl.ds(start, chunk), lanes(i, width)] = grad_state.astype(source_ref.dtype)

    transform(table_ref, source_ref, spectrum_ref)

    def state_bins(sign, real, imag):
        joined = with_next(load_bins(spectrum_ref, real, imag, count, width), sign)
        kernel = load_bins(kernel_hat_ref, real, imag, count, width)
        for i in range(count):
            total = None
            for d in range(count - i):
                total = plus(total, times_conj(kernel[d], joined[i + d]))
            store_bins(scaled_ref, real, imag, i, width, total)
        product = load_bins(product_hat_ref, real, imag, count, width)
        for d in range(count):
            total = None
            for i in range(count - d):
                total = plus(total, times_conj(product[i], joined[i + d]))
            store_bins(other_ref, real, imag, d, width, total)

    over_bins(step, state_bins)

    @pl.loop(0, step // chunk)
    def _(index):
        start = pl.multiple_of(index * chunk, chunk)
        window = pl.ds(start, chunk)
        block = jnp.dot(
            inverse_ref[window, :], other_ref[...], preferred_element_type=jnp.float32
        )
        for i in range(count):
            rows = pl.ds(pl.multiple_of(i * step + start, chunk), chunk)
            grad_kernel_ref[rows, :] = block[:, lanes(i, width)]

    @pl.loop(0, step // chunk)
    def _(index):
        start = pl.multiple_of(index * chunk, chunk)
        window = pl.ds(start, chunk)
        block = jnp.dot(
            inverse_ref[window, :], scaled_ref[...], preferred_element_type=jnp.float32
        )
        for i in range(count):
            rows = pl.ds(pl.multiple_of(i * step + start, chunk), chunk)
            grad_state = grad_ref[rows, :].astype(jnp.float32) * query_ref[rows, :].astype(
                jnp.float32
            )
            grad_product = block[:, lanes(i, width)] + skip_ref[...] * grad_state
            grad_values_ref[rows, :] = (
                grad_product * shifted_ref[rows, :].astype(jnp.float32)
            ).astype(grad_values_ref.dtype)
            source_ref[window, lanes(i, width)] = (
                grad_product * values_ref[rows, :].astype(jnp.float32)
            ).astype(source_ref.dtype)

    transform(table_ref, source_ref, spectrum_ref)

    def shift_bins(sign, real, imag):
        joined = with_next(load_bins(spectrum_ref, real, imag, count, width), sign)
        keys = load_bins(keys_hat_ref, real, imag, count, width)
        taps = (taps_hat_ref[real, :], taps_hat_ref[imag, :])
        total = None
        for i in range(count):
            store_bins(scaled_ref, real, imag, i, width, times_conj(taps, joined[i]))
            total = plus(total, times_conj(keys[i], joined[i]))
        store_bins(taps_acc_ref, real, imag, 0, width, total)

    over_bins(step, shift_bins)
    grad_taps_ref[...] = jnp.dot(
        inverse_ref[:state_taps, :], taps_acc_ref[...], preferred_element_type=jnp.float32
    )

    @pl.loop(0, step // chunk)
    def _(index):
        start = pl.multiple_of(index * chunk, chunk)
        window = pl.ds(start, chunk)
        block = jnp.dot(
            inverse_ref[window, :], scaled_ref[...], preferred_element_type=jnp.float32
        )
        for i in range(count):
            rows = pl.ds(pl.multiple_of(i * step + start, chunk), chunk)
            grad_keys_ref[rows, :] = block[:, lanes(i, width)].astype(grad_keys_ref.dtype)


def mixer_sizes(channels):
    step = min(SLOT, 512)
    width = 128 if channels % 128 == 0 else channels
    return SLOT // step, step, width


def mixer_tables(step):
    table = wave_table(step)
    high = table.astype(jnp.bfloat16)
    low = (table - high.astype(np.float64)).astype(jnp.bfloat16)
    return jnp.asarray(high), jnp.asarray(table.T / step, jnp.bfloat16), jnp.asarray(low)


def run_forward(query, keys, values, kernel, taps, skip):
    channels = keys.shape[1]
    count, step, width = mixer_sizes(channels)
    forward_table, inverse_table, low_table = mixer_tables(step)
    fixed = lambda shape: pl.BlockSpec(shape, lambda j: (0, 0), pipeline_mode=pl.Buffered(1))
    column = lambda rows: pl.BlockSpec((rows, width), lambda j: (0, j))
    wide = pl.BlockSpec((2 * step, count * width), lambda j: (0, j))
    shape = jax.ShapeDtypeStruct
    state_taps = taps.shape[0] // 2
    return pl.pallas_call(
        functools.partial(mix_forward, count, step, width),
        grid=(channels // width,),
        in_specs=[fixed((2 * step, step)), fixed((step, 2 * step)), fixed((2 * step, state_taps))]
        + [column(SLOT)] * 4
        + [column(2 * state_taps), column(1)],
        out_specs=[column(SLOT)] * 3 + [wide] * 3 + [column(2 * step)],
        out_shape=[shape((SLOT, channels), jnp.bfloat16)] * 3
        + [shape((2 * step, count * channels), jnp.bfloat16)] * 3
        + [shape((2 * step, channels), jnp.float32)],
        scratch_shapes=[
            pltpu.VMEM((step, count * width), jnp.bfloat16),
            pltpu.VMEM((2 * step, count * width), jnp.float32),
            pltpu.VMEM((2 * step, count * width), jnp.bfloat16),
            pltpu.VMEM((SLOT, width), jnp.float32),
        ],
        compiler_params=pltpu.CompilerParams(vmem_limit_bytes=48 << 20),
        name="mix_forward",
    )(forward_table, inverse_table, low_table[:, :state_taps], query, keys, values, kernel, taps, skip)


def run_backward(grad, query, values, saved, skip, state_taps):
    channels = query.shape[1]
    count, step, width = mixer_sizes(channels)
    forward_table, inverse_table, low_table = mixer_tables(step)
    fixed = lambda shape: pl.BlockSpec(shape, lambda j: (0, 0), pipeline_mode=pl.Buffered(1))
    column = lambda rows: pl.BlockSpec((rows, width), lambda j: (0, j))
    wide = pl.BlockSpec((2 * step, count * width), lambda j: (0, j))
    shape = jax.ShapeDtypeStruct
    shifted, state, keys_hat, product_hat, kernel_hat, taps_hat = saved
    return pl.pallas_call(
        functools.partial(mix_backward, count, step, width),
        grid=(channels // width,),
        in_specs=[fixed((2 * step, step)), fixed((step, 2 * step))]
        + [column(SLOT)] * 5
        + [wide] * 3
        + [column(2 * step), column(1)],
        out_specs=[column(SLOT)] * 4 + [column(state_taps), column(1)],
        out_shape=[shape((SLOT, channels), jnp.bfloat16)] * 3
        + [
            shape((SLOT, channels), jnp.float32),
            shape((state_taps, channels), jnp.float32),
            shape((1, channels), jnp.float32),
        ],
        scratch_shapes=[
            pltpu.VMEM((step, count * width), jnp.bfloat16),
            pltpu.VMEM((2 * step, count * width), jnp.float32),
            pltpu.VMEM((2 * step, count * width), jnp.bfloat16),
            pltpu.VMEM((2 * step, count * width), jnp.bfloat16),
            pltpu.VMEM((2 * step, width), jnp.bfloat16),
        ],
        compiler_params=pltpu.CompilerParams(vmem_limit_bytes=48 << 20),
        name="mix_backward",
    )(
        forward_table, inverse_table, grad, query, values, shifted, state,
        keys_hat, product_hat, kernel_hat, taps_hat, skip,
    )
MESH = pl.DeviceIdType.MESH
AXES = ("z", "y", "x")
SIDES = ((0, 1), (1, -1))


def chip_sizes(rows_axis, columns_axis):
    across = columns_axis // 2
    return {"z": rows_axis // across, "y": across, "x": across}


def chip_place(sizes):
    group, part = lax.axis_index("dp"), lax.axis_index("seq")
    return {
        "z": lax.div(group, sizes["y"]),
        "y": lax.rem(group, sizes["y"]),
        "x": lax.div(part, 2),
        "core": lax.rem(part, 2),
    }


def device_at(sizes, place):
    return {"dp": place["z"] * sizes["y"] + place["y"], "seq": place["x"] * 2 + place["core"]}


def inside(value, size):
    return jnp.logical_and(value >= 0, value < size)


def meet(sizes, place):
    barrier = pltpu.get_barrier_semaphore()
    pl.semaphore_signal(
        barrier,
        inc=1,
        device_id=device_at(sizes, {**place, "core": 1 - place["core"]}),
        device_id_type=MESH,
    )
    count = jnp.int32(1)
    for axis in AXES:
        for step in (-1, 1):
            other = place[axis] + step
            there = inside(other, sizes[axis])
            count = count + there.astype(jnp.int32)

            @pl.when(there)
            def _(axis=axis, other=other):
                pl.semaphore_signal(
                    barrier,
                    inc=1,
                    device_id=device_at(sizes, {**place, axis: other}),
                    device_id_type=MESH,
                )

    pl.semaphore_wait(barrier, count)


def plane_orders(sizes):
    return (("x", "y"), ("y", "x"))


def plane_hops(sizes):
    return sizes["x"] + sizes["y"] - 2


def plane_hop(sizes, order, number):
    done = ()
    for axis in order:
        if number < sizes[axis] - 1:
            return axis, done, number
        number -= sizes[axis] - 1
        done += (axis,)
    return None


def plane_index(place, wide, axis, value):
    return tuple(
        slice(None) if name in wide else (value if name == axis else place[name])
        for name in ("y", "x")
    )


def gather_items(sizes, count):
    return [
        (k, step, side)
        for k in range(count)
        for step in range(sizes["z"])
        for side in ((0,) if step == 0 else (0, 1))
    ]


def gather_kernel(sizes, count, *refs):
    shards, fulls = refs[:count], refs[count : 2 * count]
    send_sem, recv_sem, own_sem = refs[2 * count :]
    place = chip_place(sizes)
    core = place["core"]
    meet(sizes, place)
    items = gather_items(sizes, count)
    last = plane_hops(sizes)

    def own_copy(k):
        target = fulls[k].at[place["z"], place["y"], place["x"], core]
        return pltpu.make_async_copy(shards[k], target, own_sem.at[k])

    def remote(block, item, number, side, target):
        return pltpu.make_async_remote_copy(
            src_ref=block,
            dst_ref=block,
            send_sem=send_sem.at[item, number, side],
            recv_sem=recv_sem.at[item, number, side],
            device_id=device_at(sizes, {**place, **target}),
            device_id_type=MESH,
        )

    def layer(item):
        k, step, side = items[item]
        z = place["z"] - SIDES[side][1] * step
        return k, z, inside(z, sizes["z"])

    def along_z(item, act):
        k, z, there = layer(item)
        _, step, side = items[item]
        block = fulls[k].at[z, place["y"], place["x"], core]
        if act == "get" and step > 0:
            direction = SIDES[side][1]

            @pl.when(there)
            def _():
                remote(block, item, 0, side, {"z": place["z"] - direction}).wait_recv()

        if act in ("send", "sent") and step < sizes["z"] - 1:
            for out, direction in SIDES if step == 0 else (SIDES[side],):
                target = place["z"] + direction
                following = items.index((k, step + 1, out))

                @pl.when(jnp.logical_and(there, inside(target, sizes["z"])))
                def _():
                    copy = remote(block, following, 0, out, {"z": target})
                    copy.start() if act == "send" else copy.wait_send()

    def in_plane(item, number, act):
        k, z, there = layer(item)
        for value, order in enumerate(plane_orders(sizes)):
            axis, wide, before = plane_hop(sizes, order, number)
            here, size = place[axis], sizes[axis]
            for side, direction in SIDES:
                if act == "get":
                    held, other = here - direction * (before + 1), here - direction
                    acts = inside(held, size)
                else:
                    held, other = here - direction * before, here + direction
                    acts = jnp.logical_and(inside(held, size), inside(other, size))
                acts = jnp.logical_and(jnp.logical_and(acts, there), core == value)

                @pl.when(acts)
                def _():
                    block = fulls[k].at[(z,) + plane_index(place, wide, axis, held) + (core,)]
                    copy = remote(block, item, 1 + number, side, {axis: other})
                    if act == "send":
                        copy.start()
                    elif act == "sent":
                        copy.wait_send()
                    else:
                        copy.wait_recv()

    def across(item, act):
        k, z, there = layer(item)

        @pl.when(there)
        def _():
            owner = 1 - core if act == "get" else core
            copy = remote(fulls[k].at[z, :, :, owner], item, 1 + last, 0, {"core": 1 - core})
            if act == "send":
                copy.start()
            elif act == "sent":
                copy.wait_send()
            else:
                copy.wait_recv()

    for k in range(count):
        own_copy(k).start()
    for slot in range(len(items) + last):
        for phase in range(last + 1):
            item = slot - phase
            if not 0 <= item < len(items):
                continue
            if phase == 0:
                if items[item][1] == 0:
                    own_copy(items[item][0]).wait()
                along_z(item, "get")
                along_z(item, "send")
            else:
                in_plane(item, phase - 1, "get")
            if phase < last:
                in_plane(item, phase, "send")
            else:
                across(item, "send")
    for item in range(len(items)):
        across(item, "get")
        along_z(item, "sent")
        for number in range(last):
            in_plane(item, number, "sent")
        across(item, "sent")


def gather_all(arrays, sizes, collective_id):
    lead = tuple(sizes[axis] for axis in AXES) + (2,)
    count = len(arrays)
    hbm = pl.BlockSpec(memory_space=pl.ANY)
    semaphores = (len(gather_items(sizes, count)), plane_hops(sizes) + 2, 2)
    fulls = pl.pallas_call(
        functools.partial(gather_kernel, sizes, count),
        out_shape=[jax.ShapeDtypeStruct(lead + a.shape, a.dtype) for a in arrays],
        in_specs=[hbm] * count,
        out_specs=[hbm] * count,
        scratch_shapes=[
            pltpu.SemaphoreType.DMA(semaphores),
            pltpu.SemaphoreType.DMA(semaphores),
            pltpu.SemaphoreType.DMA((count,)),
        ],
        compiler_params=pltpu.CompilerParams(
            collective_id=collective_id, has_side_effects=True, vmem_limit_bytes=1 << 20
        ),
        name="gather_all",
    )(*arrays)
    return [f.reshape((-1,) + f.shape[5:]) for f in fulls]


def reduce_items(sizes, count):
    return [
        (k, step, side)
        for k in range(count)
        for step in reversed(range(sizes["z"]))
        for side in ((0,) if step == 0 else (0, 1))
    ]


def reduce_kernel(sizes, count, *refs):
    grads, shares = refs[:count], refs[count : 2 * count]
    rounded, sums, firsts = (refs[i * count : (i + 1) * count] for i in (2, 3, 4))
    plane_in = refs[5 * count : 6 * count]
    z_in = refs[6 * count : 7 * count]
    send_sem, recv_sem, own_sem = refs[7 * count :]
    place = chip_place(sizes)
    core = place["core"]
    meet(sizes, place)
    items = reduce_items(sizes, count)
    last = plane_hops(sizes)

    def layer(item):
        k, step, side = items[item]
        z = place["z"] + SIDES[side][1] * step
        return k, z, inside(z, sizes["z"])

    def remote(source, landing, item, number, side, target):
        return pltpu.make_async_remote_copy(
            src_ref=source,
            dst_ref=landing,
            send_sem=send_sem.at[item, number, side],
            recv_sem=recv_sem.at[item, number, side],
            device_id=device_at(sizes, {**place, **target}),
            device_id_type=MESH,
        )

    def own_copy(item):
        k, z, _ = layer(item)
        return pltpu.make_async_copy(
            grads[k].at[z, :, :, core], rounded[k].at[z], own_sem.at[item]
        )

    def across(item):
        k, z, _ = layer(item)
        return remote(
            grads[k].at[z, :, :, 1 - core], firsts[k].at[z], item, 0, 0, {"core": 1 - core}
        )

    def begin(item):
        @pl.when(layer(item)[2])
        def _():
            own_copy(item).start()
            across(item).start()

    def put(k, index, total):
        sums[k][index] = total
        rounded[k][index] = total.astype(jnp.bfloat16)

    def join_cores(item):
        k, z, there = layer(item)

        @pl.when(there)
        def _():
            own_copy(item).wait()
            across(item).wait_recv()

            @pl.loop(0, sizes["y"] * sizes["x"])
            def _(flat):
                index = (z, lax.div(flat, sizes["x"]), lax.rem(flat, sizes["x"]))
                put(
                    k,
                    index,
                    rounded[k][index].astype(jnp.float32) + firsts[k][index].astype(jnp.float32),
                )

    def in_plane(item, number, act):
        k, z, there = layer(item)
        for value, order in enumerate(plane_orders(sizes)):
            axis, wide, step = plane_hop(sizes, order, number)
            wide = tuple(name for name in order[order.index(axis) + 1 :])
            here, size = place[axis], sizes[axis]
            far = size - 1 - step
            spans = int(np.prod([sizes[name] for name in wide], dtype=np.int64))
            for side, direction in SIDES:
                if act == "get":
                    other = here - direction
                    goal = other + direction * far
                    acts = jnp.logical_and(inside(other, size), inside(goal, size))
                else:
                    other = here + direction
                    goal = here + direction * far
                    acts = inside(goal, size)
                acts = jnp.logical_and(jnp.logical_and(acts, there), core == value)

                @pl.when(acts)
                def _():
                    source = rounded[k].at[(z,) + plane_index(place, wide, axis, goal)]
                    landing = plane_in[k].at[z, number, side]
                    landing = landing.at[pl.ds(0, spans)] if wide else landing.at[0]
                    copy = remote(source, landing, item, 1 + number, side, {axis: other})
                    if act == "send":
                        copy.start()
                    elif act == "sent":
                        copy.wait_send()
                    else:
                        copy.wait_recv()

                        @pl.loop(0, spans)
                        def _(flat):
                            at = {name: flat for name in wide}
                            at[axis] = goal
                            index = (z,) + tuple(at.get(name, place[name]) for name in ("y", "x"))
                            came = plane_in[k][z, number, side, flat].astype(jnp.float32)
                            put(k, index, sums[k][index] + came)

    def along_z(item, act):
        k, z, there = layer(item)
        _, step, side = items[item]
        index = (z, place["y"], place["x"])
        if act == "get":
            for out, direction in SIDES if step == 0 else (SIDES[side],):
                other = place["z"] - direction

                @pl.when(jnp.logical_and(there, inside(other, sizes["z"])))
                def _():
                    if step + 1 < sizes["z"]:
                        leaving = items.index((k, step + 1, out))
                        remote(
                            rounded[k].at[index], z_in[k].at[out, step], leaving, 1 + last, 0,
                            {"z": other},
                        ).wait_recv()
                        put(
                            k, index, sums[k][index] + z_in[k][out, step].astype(jnp.float32)
                        )

            if step == 0:
                shares[k][...] = sums[k][index]
        elif step > 0:
            direction = SIDES[side][1]

            @pl.when(there)
            def _():
                copy = remote(
                    rounded[k].at[index], z_in[k].at[side, step - 1], item, 1 + last, 0,
                    {"z": place["z"] + direction},
                )
                copy.start() if act == "send" else copy.wait_send()

    for item in range(len(items)):
        begin(item)
    for slot in range(len(items) + last + 1):
        for phase in range(last + 2):
            item = slot - phase
            if not 0 <= item < len(items):
                continue
            if phase == 0:
                join_cores(item)
            elif phase <= last:
                in_plane(item, phase - 1, "get")
            if phase < last:
                in_plane(item, phase, "send")
            if phase == last + 1:
                along_z(item, "get")
                along_z(item, "send")
    for item in range(len(items)):

        @pl.when(layer(item)[2])
        def _():
            across(item).wait_send()

        for number in range(last):
            in_plane(item, number, "sent")
        along_z(item, "sent")


def reduce_all(arrays, sizes, collective_id):
    lead = tuple(sizes[axis] for axis in AXES)
    devices = 2 * int(np.prod(lead))
    count = len(arrays)
    blocks = [(a.shape[0] // devices, a.shape[1]) for a in arrays]
    views = [
        a.astype(jnp.bfloat16).reshape(lead + (2,) + block) for a, block in zip(arrays, blocks)
    ]
    last = plane_hops(sizes)
    widest = max(sizes["x"], sizes["y"])
    semaphores = (len(reduce_items(sizes, count)), last + 2, 2)
    return pl.pallas_call(
        functools.partial(reduce_kernel, sizes, count),
        out_shape=[jax.ShapeDtypeStruct(block, jnp.float32) for block in blocks],
        in_specs=[pl.BlockSpec(memory_space=pl.ANY)] * count,
        out_specs=[pl.BlockSpec(memory_space=pltpu.VMEM)] * count,
        scratch_shapes=[pltpu.VMEM(lead + block, jnp.bfloat16) for block in blocks]
        + [pltpu.VMEM(lead + block, jnp.float32) for block in blocks]
        + [pltpu.VMEM(lead + block, jnp.bfloat16) for block in blocks]
        + [pltpu.VMEM((sizes["z"], last, 2, widest) + block, jnp.bfloat16) for block in blocks]
        + [pltpu.VMEM((2, sizes["z"]) + block, jnp.bfloat16) for block in blocks]
        + [
            pltpu.SemaphoreType.DMA(semaphores),
            pltpu.SemaphoreType.DMA(semaphores),
            pltpu.SemaphoreType.DMA((semaphores[0],)),
        ],
        compiler_params=pltpu.CompilerParams(
            collective_id=collective_id, has_side_effects=True, vmem_limit_bytes=60 << 20
        ),
        name="reduce_all",
    )(*views)


def powers(rate, turn, count, stride):
    places = (jnp.arange(count) * stride).astype(jnp.float32)
    fade = jnp.exp(-rate[:, :, None] * places)
    angle = turn[:, :, None] * places
    return fade * jnp.cos(angle), fade * jnp.sin(angle)


def mode_kernel(rate, turn, coef):
    coarse_re, coarse_im = powers(rate, turn, SLOT // FINE, FINE)
    fine_re, fine_im = powers(rate, turn, FINE, 1)
    first, second = coef[:, 0, :, None], coef[:, 1, :, None]
    left = jnp.concatenate(
        [first * coarse_re - second * coarse_im, -first * coarse_im - second * coarse_re], axis=1
    )
    right = jnp.concatenate([fine_re, fine_im], axis=1)
    kernel = jnp.einsum("cna,cnb->cab", left, right, precision=highest)
    return kernel.reshape(rate.shape[0], SLOT)


def mode_grads(rate, turn, coef, grad_kernel):
    modes = rate.shape[1]
    coarse_re, coarse_im = powers(rate, turn, SLOT // FINE, FINE)
    fine_re, fine_im = powers(rate, turn, FINE, 1)
    inner = jnp.arange(FINE).astype(jnp.float32)
    right = jnp.concatenate([fine_re, fine_im, inner * fine_re, inner * fine_im], axis=1)
    blocks = grad_kernel.reshape(rate.shape[0], SLOT // FINE, FINE)
    sums = jnp.einsum("cab,cnb->cna", blocks, right, precision=highest)
    low_re, low_im, slope_re, slope_im = (
        sums[:, i * modes : (i + 1) * modes] for i in range(4)
    )
    outer = (jnp.arange(SLOT // FINE) * FINE).astype(jnp.float32)
    slope_re, slope_im = outer * low_re + slope_re, outer * low_im + slope_im
    zero_re = jnp.sum(coarse_re * low_re - coarse_im * low_im, axis=2)
    zero_im = jnp.sum(coarse_re * low_im + coarse_im * low_re, axis=2)
    one_re = jnp.sum(coarse_re * slope_re - coarse_im * slope_im, axis=2)
    one_im = jnp.sum(coarse_re * slope_im + coarse_im * slope_re, axis=2)
    first, second = coef[:, 0], coef[:, 1]
    grad_coef = jnp.stack([zero_re, -zero_im], axis=1)
    grad_rate = -(first * one_re - second * one_im)
    grad_turn = -(first * one_im + second * one_re)
    return grad_rate, grad_turn, grad_coef


def two_parts(values):
    high = values.astype(jnp.bfloat16)
    return high, (values - high.astype(jnp.float32)).astype(jnp.bfloat16)


def local(
    tokens,
    cotangent,
    lengths,
    norm_gains,
    shift_taps,
    decay_rate,
    frequency,
    mode_coef,
    skip_gain,
    qkv_weight,
    out_weight,
    up_weight,
    down_weight,
):
    parts = lax.axis_size("seq")
    slots, length, width = tokens.shape
    half = parts // slots
    place = lax.axis_index("seq")
    slot, rank = place // half, place % half
    channels = width // half
    state_taps = shift_taps.shape[1]
    sizes = chip_sizes(lax.axis_size("dp"), parts)

    def swap(values):
        return lax.ppermute(values, "seq", [(i, (i + half) % parts) for i in range(parts)])

    def pick(pair, index):
        return lax.dynamic_index_in_dim(pair, index, 0, keepdims=False)

    def rows_of(pair):
        kept, came = pick(pair, slot), swap(pick(pair, 1 - slot))
        low = jnp.where(slot == 0, kept, came)
        high = jnp.where(slot == 0, came, kept)
        return jnp.concatenate([low, high], axis=0)

    def home_of(rows, dtype):
        pair = rows.reshape(2, length, width)
        kept = pick(pair, slot).astype(dtype)
        came = swap(pick(pair, 1 - slot).astype(jnp.bfloat16)).astype(dtype)
        return jnp.stack(
            [jnp.where(slot == 0, kept, came), jnp.where(slot == 0, came, kept)], axis=0
        )

    token_rows = rows_of(tokens)
    gain_high, gain_low = two_parts(norm_gains)
    skip_high, skip_low = two_parts(skip_gain[:, None])
    taps_high, taps_low = two_parts(shift_taps)
    kernel_own = mode_kernel(decay_rate, frequency, mode_coef)
    small = jnp.concatenate(
        [
            kernel_own.astype(jnp.bfloat16),
            taps_high,
            taps_low,
            gain_high,
            gain_low,
            skip_high,
            skip_low,
            jnp.zeros((kernel_own.shape[0], 128 - 6), jnp.bfloat16),
        ],
        axis=1,
    )
    qkv_full, small_full, out_full, up_full, down_full = gather_all(
        [qkv_weight, small, out_weight, up_weight, down_weight],
        sizes,
        0,
    )
    cotangent, down_full = lax.optimization_barrier((cotangent, down_full))
    cot_rows = rows_of(cotangent)
    base = SLOT + state_taps
    extra = small_full[:, base + state_taps : base + state_taps + 6].astype(jnp.float32)
    gain_one, gain_two = extra[:, 0] + extra[:, 2], extra[:, 1] + extra[:, 3]
    start = rank * channels
    mine = lax.dynamic_slice_in_dim(small_full, start, channels, 0)
    kernel_mine = mine[:, :SLOT].T
    taps_mine = mine[:, SLOT : base + state_taps].T
    skip_mine = lax.dynamic_slice_in_dim(extra[:, 4] + extra[:, 5], start, channels, 0)[None, :]

    input_rows = token_rows.astype(jnp.float32)
    normed_one, norm_one_back = jax.vjp(layer_norm, input_rows, gain_one)
    normed_low = normed_one.astype(jnp.bfloat16)
    projected = mat_dot(normed_low, qkv_full, ((1,), (0,))).astype(jnp.bfloat16)

    def shift_rank(values, k):
        pairs = [(i, i // half * half + (i % half + k) % half) for i in range(parts)]
        return lax.ppermute(values, "seq", pairs)

    def to_channels(values, fold):
        rows = values.shape[0]
        by_rank = values.reshape(rows, fold, half, channels)
        pieces = []
        for k in range(half):
            piece = lax.dynamic_index_in_dim(by_rank, (rank + k) % half, 2, keepdims=False)
            pieces.append(piece if k == 0 else shift_rank(piece, k))
        ordered = jnp.stack(
            [
                lax.select_n((rank - i) % half, *pieces) if half > 1 else pieces[0]
                for i in range(half)
            ],
            axis=0,
        )
        ordered = ordered.reshape(half, 2, length, fold, channels)
        return ordered.transpose(1, 0, 2, 3, 4).reshape(SLOT, fold, channels)

    def to_rows(values, fold):
        by_rank = values.reshape(2, half, length, fold, channels)
        pieces = []
        for k in range(half):
            piece = lax.dynamic_index_in_dim(by_rank, (rank + k) % half, 1, keepdims=False)
            piece = piece.reshape(2 * length, fold, channels)
            pieces.append(piece if k == 0 else shift_rank(piece, k))
        ordered = [
            lax.select_n((rank - i) % half, *pieces) if half > 1 else pieces[0]
            for i in range(half)
        ]
        return jnp.concatenate(ordered, axis=2).reshape(2 * length, fold * width)

    triple = to_channels(projected, 3)
    query, keys, values = triple[:, 0], triple[:, 1], triple[:, 2]
    mixed, *saved = run_forward(query, keys, values, kernel_mine, taps_mine, skip_mine)
    mixed_rows = to_rows(mixed, 1)
    hidden = input_rows + mat_dot(mixed_rows, out_full, ((1,), (0,)))
    normed_two, norm_two_back = jax.vjp(layer_norm, hidden, gain_two)
    normed_two_low = normed_two.astype(jnp.bfloat16)
    pre_act = mat_dot(normed_two_low, up_full, ((1,), (0,)))
    activity, gelu_back = jax.vjp(exact_gelu, pre_act)
    activity_low = activity.astype(jnp.bfloat16)
    reach = lax.dynamic_index_in_dim(
        lengths, lax.axis_index("dp") * slots + slot, 0, keepdims=False
    )
    ids = rank * length + jnp.arange(length, dtype=jnp.int32)
    ids = jnp.concatenate([ids, ids + SLOT // 2])
    live_mask = (ids < reach).astype(jnp.float32)[:, None]
    result_rows = live_mask * (hidden + mat_dot(activity_low, down_full, ((1,), (0,))))
    layer_out = home_of(result_rows, jnp.bfloat16)

    grad_sum = live_mask * cot_rows.astype(jnp.float32)
    grad_branch = grad_sum.astype(jnp.bfloat16)
    down_grad = mat_dot(activity_low, grad_branch, ((0,), (0,)))
    grad_act = mat_dot(grad_branch, down_full, ((1,), (1,)))
    grad_pre = gelu_back(grad_act)[0].astype(jnp.bfloat16)
    up_grad = mat_dot(normed_two_low, grad_pre, ((0,), (0,)))
    grad_normed = mat_dot(grad_pre, up_full, ((1,), (1,)))
    grad_hidden_norm, grad_gain_two = norm_two_back(grad_normed)
    grad_hidden = grad_sum + grad_hidden_norm
    up_share, down_share = reduce_all([up_grad, down_grad], sizes, 1)
    grad_mix = grad_hidden.astype(jnp.bfloat16)
    out_grad = mat_dot(mixed_rows, grad_mix, ((0,), (0,)))
    grad_mixed = mat_dot(grad_mix, out_full, ((1,), (1,))).astype(jnp.bfloat16)
    channel_grad = to_channels(grad_mixed, 1)[:, 0]
    grad_query, grad_keys, grad_values, grad_kernel, grad_taps, grad_skip = run_backward(
        channel_grad, query, values, saved, skip_mine, state_taps
    )
    grad_projected = to_rows(jnp.stack([grad_query, grad_keys, grad_values], axis=1), 3)
    qkv_grad = mat_dot(normed_low, grad_projected, ((0,), (0,)))
    grad_normed_one = mat_dot(grad_projected, qkv_full, ((1,), (1,)))
    grad_input_norm, grad_gain_one = norm_one_back(grad_normed_one)
    input_grad = home_of(grad_hidden + grad_input_norm, jnp.float32)

    packed = jnp.concatenate([grad_kernel, grad_taps, grad_skip], axis=0).T
    wide = lax.dynamic_update_slice_in_dim(
        jnp.zeros((width, packed.shape[1]), jnp.float32), packed, start, 0
    )
    wide = jnp.concatenate([wide, grad_gain_one[:, None], grad_gain_two[:, None]], axis=1)
    wide = jnp.pad(wide, ((0, 0), (0, -wide.shape[1] % 128)))
    out_share, small_share, qkv_share = reduce_all(
        [out_grad, wide, qkv_grad], sizes, 2
    )
    grad_rate, grad_turn, grad_coef = mode_grads(
        decay_rate, frequency, mode_coef, small_share[:, :SLOT]
    )
    return (
        layer_out,
        input_grad,
        small_share[:, base + 1 : base + 3],
        small_share[:, SLOT:base],
        grad_rate,
        grad_turn,
        grad_coef,
        small_share[:, base],
        qkv_share,
        out_share,
        up_share,
        down_share,
    )


def solution(mesh):
    return jax.shard_map(
        local,
        mesh=mesh,
        in_specs=(
            P("dp", "seq", None),
            P("dp", "seq", None),
            P(),
            P(("dp", "seq"), None),
            P(("dp", "seq"), None),
            P(("dp", "seq"), None),
            P(("dp", "seq"), None),
            P(("dp", "seq"), None, None),
            P(("dp", "seq")),
            P(("dp", "seq"), None),
            P(("dp", "seq"), None),
            P(("dp", "seq"), None),
            P(("dp", "seq"), None),
        ),
        out_specs=(
            P("dp", "seq", None),
            P("dp", "seq", None),
            P(("dp", "seq"), None),
            P(("dp", "seq"), None),
            P(("dp", "seq"), None),
            P(("dp", "seq"), None),
            P(("dp", "seq"), None, None),
            P(("dp", "seq")),
            P(("dp", "seq"), None),
            P(("dp", "seq"), None),
            P(("dp", "seq"), None),
            P(("dp", "seq"), None),
        ),
        check_vma=False,
    )
```
